32 devices in a mesh: lat: 4 (over y, x), kpt: 8 (over z, core).
Axes of the slice: x: 2, y: 2, z: 4, core: 2. Of those that a mesh axis runs over, the one named last changes fastest.
Arguments:
- coarse: bfloat16 [2, 4, 32, 12288], P(None, 'lat', 'kpt'), may hold values from -1 to 1
- rp_vectors: int32 [4, 3], P('lat'), may hold values from -4 to 4
- rp_weights: int32 [4], P('lat'), may hold values from 1 to 3
- re_vectors: int32 [32, 3], replicated, may hold values from -4 to 4
- re_weights: int32 [32], replicated, may hold values from 1 to 3
- q_points: float32 [2, 3], replicated, may hold values from 0 to 1
- k_points: float32 [512, 3], P('kpt'), may hold values from 0 to 1
- modes_rot: bfloat16 [2, 2, 48, 48], replicated, may hold values from -0.625 to 0.625
- u_k: bfloat16 [2, 512, 16, 16], P(None, 'kpt'), may hold values from -1 to 1
- u_kq: bfloat16 [2, 2, 512, 16, 16], P(None, None, 'kpt'), may hold values from -1 to 1
- mask_k: int32 [512, 16], P('kpt'), may hold values 0 or 1
- mask_kq: int32 [2, 512, 16], P(None, 'kpt'), may hold values 0 or 1
Outputs:
- coupling: bfloat16 [2, 512, 2, 12288], P(None, 'kpt', None, 'lat')
The draws below stay inside these ranges and needn't reach their ends.
All inputs are finite; a program needn't handle non-finite values. No bound on the sum of `mask_k` or of `mask_kq` on one device may be relied on, other than what follows from the above.
Results may differ from the reference program's by a relative error of at most 0.017.
Values may be sent and summed in bfloat16 or wider, within the bound.
A program may use at most 128 MiB of HBM per device.

```python
import jax
import jax.numpy as jnp
from jax import lax

W = 16
M = 48
NQ = 2
NK = 512
NRP = 4
NRE = 32


def touch_ends(entries, stream_key, least, largest):
    index_at = [jax.random.randint(jax.random.fold_in(stream_key, axis), (), 0, length) for axis, length in enumerate(entries.shape)]
    longest = entries.shape.index(max(entries.shape))
    neighbour = index_at[:longest] + [(index_at[longest] + 1) % entries.shape[longest]] + index_at[longest + 1:]
    return entries.at[tuple(index_at)].set(least).at[tuple(neighbour)].set(largest)


def steps_of(key, extent, cuts, least, top_value):
    def one(dim, shards_of):
        steps = jax.random.uniform(jax.random.fold_in(jax.random.fold_in(key, 6), dim), (shards_of,), jnp.float32, least / len(cuts), top_value / len(cuts))
        return jnp.repeat(jnp.exp(steps), extent[dim] // shards_of).reshape((-1,) + (1,) * (len(extent) - dim - 1))

    gain = one(*cuts[0])
    for cut in cuts[1:]:
        gain = gain * one(*cut)
    return gain


def scatter_about(stream_key, shape, scale, reach, split=(), dtype=jnp.bfloat16):
    drawn = jax.random.normal(stream_key, shape, jnp.float32) * scale
    if len(split) > 0:
        drawn = steps_of(stream_key, shape, split, -0.22, 0.18) * drawn
    return jnp.clip(drawn, min=-reach, max=reach).astype(dtype)


def setup_inputs(seed: int = 0) -> dict:
    arg_keys = jax.random.split(jax.random.key(seed), 13)
    return {
        "coarse": scatter_about(arg_keys[0], (2, NRP, NRE, M * W * W), (NRP * NRE // 4) ** -0.5, 1.0, ((1, 4), (2, 8))),
        "rp_vectors": touch_ends(jax.random.randint(arg_keys[1], (NRP, 3), -4, 5), jax.random.fold_in(arg_keys[1], 1), -4, 4).astype(jnp.int32),
        "rp_weights": touch_ends(jax.random.randint(arg_keys[2], (NRP,), 1, 4), jax.random.fold_in(arg_keys[2], 1), 1, 3).astype(jnp.int32),
        "re_vectors": touch_ends(jax.random.randint(arg_keys[3], (NRE, 3), -4, 5), jax.random.fold_in(arg_keys[3], 1), -4, 4).astype(jnp.int32),
        "re_weights": touch_ends(jax.random.randint(arg_keys[4], (NRE,), 1, 4), jax.random.fold_in(arg_keys[4], 1), 1, 3).astype(jnp.int32),
        "q_points": jnp.clip(jax.random.uniform(arg_keys[5], (NQ, 3), jnp.float32, 0.0, 1.0), 0.0, 1.0),
        "k_points": jnp.clip(1.0 * jax.random.uniform(arg_keys[6], (NK, 3), jnp.float32) ** steps_of(arg_keys[6], (NK, 3), ((0, 8),), -0.2, 0.2), 0.0, 1.0),
        "modes_rot": scatter_about(arg_keys[7], (2, NQ, M, M), (2 * M) ** -0.5, 0.625),
        "u_k": scatter_about(arg_keys[8], (2, NK, W, W), (2 * W) ** -0.5, 1.0, ((1, 8),)),
        "u_kq": scatter_about(arg_keys[9], (2, NQ, NK, W, W), (2 * W) ** -0.5, 1.0, ((2, 8),)),
        "mask_k": touch_ends((jax.random.randint(arg_keys[10], (NK, W), 0, 4) < 3).astype(jnp.int32), jax.random.fold_in(arg_keys[10], 1), 0, 1),
        "mask_kq": touch_ends((jax.random.randint(arg_keys[11], (NQ, NK, W), 0, 4) < 3).astype(jnp.int32), jax.random.fold_in(arg_keys[11], 1), 0, 1),
    }


two_pi = 6.283185307179586


def phases(points, vectors, weights):
    cells = vectors.astype(jnp.float32)
    argument = two_pi * (points[:, 0:1] * cells[None, :, 0] + points[:, 1:2] * cells[None, :, 1] + points[:, 2:3] * cells[None, :, 2])
    inverse = 1.0 / weights.astype(jnp.float32)
    return (jnp.cos(argument) * inverse).astype(jnp.bfloat16), (jnp.sin(argument) * inverse).astype(jnp.bfloat16)


def reference(coarse, rp_vectors, rp_weights, re_vectors, re_weights, q_points, k_points, modes_rot, u_k, u_kq, mask_k, mask_kq):
    high = lax.Precision.HIGHEST
    phase_real, phase_imag = phases(q_points, rp_vectors, rp_weights)
    flat_real = coarse[0].reshape(NRP, NRE * M * W * W)
    flat_imag = coarse[1].reshape(NRP, NRE * M * W * W)
    part_real = jnp.dot(phase_real, flat_real, preferred_element_type=jnp.float32) - jnp.dot(phase_imag, flat_imag, preferred_element_type=jnp.float32)
    part_imag = jnp.dot(phase_real, flat_imag, preferred_element_type=jnp.float32) + jnp.dot(phase_imag, flat_real, preferred_element_type=jnp.float32)
    on_q = jnp.stack([part_real, part_imag]).astype(jnp.bfloat16)
    values = lax.optimization_barrier(on_q).astype(jnp.float32).reshape(2, NQ, NRE, M, W * W)
    eigen = modes_rot.astype(jnp.float32)
    br = jnp.einsum("qmn,qrmx->qrnx", eigen[0], values[0], precision=high) - jnp.einsum("qmn,qrmx->qrnx", eigen[1], values[1], precision=high)
    bi = jnp.einsum("qmn,qrmx->qrnx", eigen[0], values[1], precision=high) + jnp.einsum("qmn,qrmx->qrnx", eigen[1], values[0], precision=high)
    branch = jnp.stack([br, bi]).reshape(2, NQ, NRE, M * W * W).astype(jnp.bfloat16)
    kreal, kimag = phases(k_points, re_vectors, re_weights)
    kreal = kreal.astype(jnp.float32)
    kimag = kimag.astype(jnp.float32)
    grid = lax.optimization_barrier(branch).astype(jnp.float32)
    er = jnp.einsum("kr,qrx->kqx", kreal, grid[0], precision=high) - jnp.einsum("kr,qrx->kqx", kimag, grid[1], precision=high)
    ei = jnp.einsum("kr,qrx->kqx", kreal, grid[1], precision=high) + jnp.einsum("kr,qrx->kqx", kimag, grid[0], precision=high)
    bloch = jnp.stack([er, ei]).astype(jnp.bfloat16)
    field = lax.optimization_barrier(bloch).astype(jnp.float32).reshape(2, NK, NQ, M, W, W)
    right = u_k.astype(jnp.float32)
    left = u_kq.astype(jnp.float32)
    tr = jnp.einsum("kqmab,kbn->kqman", field[0], right[0], precision=high) - jnp.einsum("kqmab,kbn->kqman", field[1], right[1], precision=high)
    ti = jnp.einsum("kqmab,kbn->kqman", field[0], right[1], precision=high) + jnp.einsum("kqmab,kbn->kqman", field[1], right[0], precision=high)
    half = lax.optimization_barrier(jnp.stack([tr, ti]).astype(jnp.bfloat16)).astype(jnp.float32)
    tr = half[0]
    ti = half[1]
    outr = jnp.einsum("qkac,kqman->kqmcn", left[0], tr, precision=high) + jnp.einsum("qkac,kqman->kqmcn", left[1], ti, precision=high)
    outi = jnp.einsum("qkac,kqman->kqmcn", left[0], ti, precision=high) - jnp.einsum("qkac,kqman->kqmcn", left[1], tr, precision=high)
    window = jnp.transpose(mask_kq.astype(jnp.float32), (1, 0, 2))[:, :, None, :, None] * mask_k.astype(jnp.float32)[:, None, None, None, :]
    result = jnp.stack([outr * window, outi * window])
    return result.reshape(2, NK, NQ, M * W * W).astype(jnp.bfloat16)
```

```python
import functools

import jax
import jax.numpy as jnp
from jax import lax
from jax.experimental import pallas as pl
from jax.experimental.pallas import tpu as pltpu
from jax.sharding import PartitionSpec as P

two_pi = 6.283185307179586
f32 = jnp.float32
bf16 = jnp.bfloat16


def phases(points, vectors, weights):
    cells = vectors.astype(f32)
    argument = two_pi * (
        points[None, :, 0] * cells[:, 0:1]
        + points[None, :, 1] * cells[:, 1:2]
        + points[None, :, 2] * cells[:, 2:3]
    )
    inverse = (1.0 / weights.astype(f32))[:, None]
    return (
        (jnp.cos(argument) * inverse).astype(bf16),
        (jnp.sin(argument) * inverse).astype(bf16),
    )


def rotate_kernel(lanes, width, x_ref, rot_ref, out_ref, rows_ref):
    count = lanes // width
    sums = out_rows = rows_ref.shape[0] // count
    tail = x_ref[:, lanes:].astype(f32).T[: max(8, sums)].astype(bf16)
    total = jnp.dot(tail, x_ref[:, :lanes], preferred_element_type=f32)
    for row in range(out_rows):
        for m in range(count):
            rows_ref[pl.ds(row * count + m, 1), :] = total[row : row + 1, m * width : (m + 1) * width]
    out_ref[...] = jnp.dot(
        rot_ref[...], rows_ref[...].astype(bf16), preferred_element_type=f32
    ).astype(bf16)


def couple_kernel(cells, modes, rows, bands, p_ref, ph_ref, u1_ref, u2_ref, v1_ref, v2_ref, out_ref, wide, b1, b2, h1, h2, res):
    q = pl.program_id(0)
    m = pl.program_id(1)
    half_lanes = b1.shape[1] // 2

    @pl.when((q == 0) & (m == 0))
    def _():
        for t in range(wide.shape[0]):
            wide[t] = p_ref[:, t * 128 : (t + 1) * 128].astype(f32)

    start = q * (2 * modes) + m
    parts = [
        jnp.concatenate(
            [
                wide.at[t][pl.ds(start + c * modes, cells, stride=rows), :]
                for t in range(wide.shape[0])
            ],
            axis=1,
        )
        for c in range(2)
    ]
    pair = jnp.concatenate(parts, axis=0).astype(bf16)
    field = lax.dot_general(pair, ph_ref[...], (((0,), (0,)), ((), ())), preferred_element_type=f32)
    b1[...] = field
    b2[...] = pltpu.roll(field, half_lanes, 1)
    lanes = b1.shape[1]
    group = 4

    def step_half(g, carry):
        base = g * (group * bands)
        acc = [jnp.zeros((bands, lanes), f32) for _ in range(group)]
        for b in range(bands):
            w1 = u1_ref[b * bands : (b + 1) * bands, :]
            w2 = u2_ref[b * bands : (b + 1) * bands, :]
            for j in range(group):
                r1 = b1[pl.ds(base + j * bands + b, 1), :]
                r2 = b2[pl.ds(base + j * bands + b, 1), :]
                acc[j] = acc[j] + (w1 * r1 + w2 * r2)
        for j in range(group):
            rows_at = pl.ds(pl.multiple_of(base + j * bands, bands), bands)
            h1[rows_at, :] = acc[j]
            h2[rows_at, :] = pltpu.roll(acc[j], half_lanes, 1)
        return carry

    lax.fori_loop(0, bands // group, step_half, 0)

    def step_out(g, carry):
        base = g * group
        acc = [jnp.zeros((bands, lanes), f32) for _ in range(group)]
        for a in range(bands):
            w1 = h1[a * bands : (a + 1) * bands, :]
            w2 = h2[a * bands : (a + 1) * bands, :]
            for j in range(group):
                r1 = v1_ref[0, pl.ds(a * bands + base + j, 1), :]
                r2 = v2_ref[0, pl.ds(a * bands + base + j, 1), :]
                acc[j] = acc[j] + (w1 * r1 + w2 * r2)
        for j in range(group):
            res[pl.ds(pl.multiple_of((base + j) * bands, bands), bands), :] = acc[j]
        return carry

    lax.fori_loop(0, bands // group, step_out, 0)
    out_ref[0] = res[...].T.astype(bf16)


def per_device(
    lat_count,
    kpt_count,
    coarse,
    rp_vectors,
    rp_weights,
    re_vectors,
    re_weights,
    q_points,
    k_points,
    modes_rot,
    u_k,
    u_kq,
    mask_k,
    mask_kq,
):
    q_count = q_points.shape[0]
    k_count = k_points.shape[0]
    bands = u_k.shape[2]
    width = bands * bands
    lanes = coarse.shape[3]
    mode_count = lanes // width
    modes = mode_count // lat_count
    cells = re_vectors.shape[0]
    rows = 2 * q_count * modes
    assert coarse.shape[1] == 1 and coarse.shape[2] == lat_count

    pr, pi = phases(q_points, rp_vectors, rp_weights)
    tail = jnp.concatenate(
        [jnp.concatenate([pr, pi], 1), jnp.concatenate([-pi, pr], 1)], 0
    )
    tail = jnp.pad(tail, ((0, 0), (0, 128 - 2 * q_count)))
    block = jnp.transpose(coarse[:, 0], (1, 0, 2))
    sent = jnp.concatenate([block, jnp.broadcast_to(tail[None], (lat_count, 2, 128))], 2)
    got = lax.all_to_all(sent, "lat", split_axis=0, concat_axis=0, tiled=True)
    got = got.reshape(2 * lat_count, lanes + 128)

    rr, ri = modes_rot[0], modes_rot[1]
    turn = jnp.stack([jnp.stack([rr, -ri]), jnp.stack([ri, rr])])
    turn = turn.reshape(2, 2, q_count, mode_count, lat_count, modes)
    same = jnp.eye(q_count, dtype=bf16)
    turn = turn[:, :, :, :, :, :, None] * same[None, None, :, None, None, None, :]
    turn = jnp.transpose(turn, (4, 6, 0, 5, 1, 2, 3)).reshape(
        lat_count * rows, 2 * q_count * mode_count
    )
    branch = pl.pallas_call(
        functools.partial(rotate_kernel, lanes, width),
        out_shape=jax.ShapeDtypeStruct((lat_count * rows, width), bf16),
        scratch_shapes=[pltpu.VMEM((2 * q_count * mode_count, width), f32)],
    )(got, turn)
    branch = branch.reshape(lat_count, rows, width)
    shared = lax.all_to_all(branch, "lat", split_axis=0, concat_axis=0, tiled=True)
    portion = lax.all_gather(shared, "kpt", axis=0, tiled=True).reshape(cells * rows, width)

    kr, ki = phases(k_points, re_vectors, re_weights)
    ph = jnp.concatenate(
        [jnp.concatenate([kr, ki], 1), jnp.concatenate([-ki, kr], 1)], 0
    )
    uk = jnp.transpose(u_k.astype(f32) * mask_k.astype(f32)[None, :, None, :], (0, 2, 3, 1))
    uk = uk.reshape(2, width, k_count)
    u1 = jnp.concatenate([uk[0], uk[0]], 1)
    u2 = jnp.concatenate([-uk[1], uk[1]], 1)
    ukq = jnp.transpose(u_kq.astype(f32) * mask_kq.astype(f32)[None, :, :, None, :], (0, 1, 3, 4, 2))
    ukq = ukq.reshape(2, q_count, width, k_count)
    v1 = jnp.concatenate([ukq[0], ukq[0]], 2)
    v2 = jnp.concatenate([ukq[1], -ukq[1]], 2)

    wide_lanes = 2 * k_count
    whole = lambda q, m: (0, 0)
    result = pl.pallas_call(
        functools.partial(couple_kernel, cells, modes, rows, bands),
        grid=(q_count, modes),
        in_specs=[
            pl.BlockSpec((cells * rows, width), whole),
            pl.BlockSpec((2 * cells, wide_lanes), whole),
            pl.BlockSpec((width, wide_lanes), whole),
            pl.BlockSpec((width, wide_lanes), whole),
            pl.BlockSpec((1, width, wide_lanes), lambda q, m: (q, 0, 0)),
            pl.BlockSpec((1, width, wide_lanes), lambda q, m: (q, 0, 0)),
        ],
        out_specs=pl.BlockSpec((1, wide_lanes, width), lambda q, m: (q, 0, m)),
        out_shape=jax.ShapeDtypeStruct((q_count, wide_lanes, modes * width), bf16),
        scratch_shapes=[pltpu.VMEM((width // 128, cells * rows, 128), f32)]
        + [pltpu.VMEM((width, wide_lanes), f32)] * 5,
    )(portion, ph, u1, u2, v1, v2)
    result = result.reshape(q_count, 2, k_count, modes * width)
    return jnp.transpose(result, (1, 2, 0, 3))


def solution(mesh):
    placed = (
        P(None, "lat", "kpt", None),
        P("lat", None),
        P("lat"),
        P(),
        P(),
        P(),
        P("kpt", None),
        P(),
        P(None, "kpt", None, None),
        P(None, None, "kpt", None, None),
        P("kpt", None),
        P(None, "kpt", None),
    )
    return jax.shard_map(
        functools.partial(per_device, mesh.shape["lat"], mesh.shape["kpt"]),
        mesh=mesh,
        in_specs=placed,
        out_specs=P(None, "kpt", None, "lat"),
        check_vma=False,
    )
```

```python
import functools

import jax
import jax.numpy as jnp
from jax import lax
from jax.experimental import pallas as pl
from jax.experimental.pallas import tpu as pltpu
from jax.sharding import PartitionSpec as P

two_pi = 6.283185307179586
f32 = jnp.float32
bf16 = jnp.bfloat16


def phases(points, vectors, weights):
    cells = vectors.astype(f32)
    argument = two_pi * (
        points[None, :, 0] * cells[:, 0:1]
        + points[None, :, 1] * cells[:, 1:2]
        + points[None, :, 2] * cells[:, 2:3]
    )
    inverse = (1.0 / weights.astype(f32))[:, None]
    return (
        (jnp.cos(argument) * inverse).astype(bf16),
        (jnp.sin(argument) * inverse).astype(bf16),
    )


def rotate_kernel(lanes, width, x_ref, rot_ref, out_ref, rows_ref):
    count = lanes // width
    sums = out_rows = rows_ref.shape[0] // count
    tail = x_ref[:, lanes:].astype(f32).T[: max(8, sums)].astype(bf16)
    total = jnp.dot(tail, x_ref[:, :lanes], preferred_element_type=f32)
    for row in range(out_rows):
        for m in range(count):
            rows_ref[pl.ds(row * count + m, 1), :] = total[row : row + 1, m * width : (m + 1) * width]
    out_ref[...] = jnp.dot(
        rot_ref[...], rows_ref[...].astype(bf16), preferred_element_type=f32
    ).astype(bf16)


def push(stack, value):
    level = 0
    while stack and stack[-1][0] == level:
        value = stack.pop()[1] + value
        level += 1
    stack.append((level, value))


def couple_kernel(cells, modes, rows, bands, p_ref, ph_ref, u1_ref, u2_ref, v1_ref, v2_ref, out_ref, wide, b1, b2, h1, h2, res, c1, c2):
    q = pl.program_id(0)
    m = pl.program_id(1)
    lanes = b1.shape[1]
    half_lanes = lanes // 2

    def tile(index):
        return pl.ds(pl.multiple_of(index * bands, bands), bands)

    @pl.when((q == 0) & (m == 0))
    def _():
        for t in range(wide.shape[0]):
            wide[t] = p_ref[:, t * 128 : (t + 1) * 128].astype(f32)

    @pl.when(m == 0)
    def _():
        def spread(g, carry):
            for j in range(bands):
                r = g * bands + j
                c1[tile(r), :] = jnp.broadcast_to(v1_ref[0, pl.ds(r, 1), :], (bands, lanes)).astype(bf16)
                c2[tile(r), :] = jnp.broadcast_to(v2_ref[0, pl.ds(r, 1), :], (bands, lanes)).astype(bf16)
            return carry

        lax.fori_loop(0, bands, spread, 0)

    start = q * (2 * modes) + m
    parts = [
        jnp.concatenate(
            [
                wide.at[t][pl.ds(start + c * modes, cells, stride=rows), :]
                for t in range(wide.shape[0])
            ],
            axis=1,
        )
        for c in range(2)
    ]
    pair = jnp.concatenate(parts, axis=0).astype(bf16)
    field = lax.dot_general(pair, ph_ref[...], (((0,), (0,)), ((), ())), preferred_element_type=f32)
    b1[...] = field
    b2[...] = pltpu.roll(field, half_lanes, 1)
    group = 4

    def step_half(g, carry):
        base = g * (group * bands)
        acc = [[] for _ in range(group)]
        for b in range(bands):
            w1 = u1_ref[b * bands : (b + 1) * bands, :]
            w2 = u2_ref[b * bands : (b + 1) * bands, :]
            for j in range(group):
                r = base + j * bands + b
                r1 = jnp.broadcast_to(b1[pl.ds(r, 1), :], (bands, lanes)).astype(bf16)
                r2 = jnp.broadcast_to(b2[pl.ds(r, 1), :], (bands, lanes)).astype(bf16)
                push(acc[j], w1 * r1 + w2 * r2)
        for j in range(group):
            total = acc[j][0][1]
            h1[tile(g * group + j), :] = total
            h2[tile(g * group + j), :] = pltpu.roll(total.astype(f32), half_lanes, 1).astype(bf16)
        return carry

    lax.fori_loop(0, bands // group, step_half, 0)
    batch = 8

    def step_out(g, carry):
        base = g * batch
        acc = [[] for _ in range(batch)]
        for a in range(bands):
            w1 = h1[a * bands : (a + 1) * bands, :]
            w2 = h2[a * bands : (a + 1) * bands, :]
            for j in range(batch):
                at = tile(a * bands + base + j)
                push(acc[j], w1 * c1[at, :] + w2 * c2[at, :])
        for j in range(batch):
            res[tile(base + j), :] = acc[j][0][1].astype(f32)
        return carry

    lax.fori_loop(0, bands // batch, step_out, 0)
    out_ref[0] = res[...].T.astype(bf16)


def per_device(
    lat_count,
    kpt_count,
    coarse,
    rp_vectors,
    rp_weights,
    re_vectors,
    re_weights,
    q_points,
    k_points,
    modes_rot,
    u_k,
    u_kq,
    mask_k,
    mask_kq,
):
    q_count = q_points.shape[0]
    k_count = k_points.shape[0]
    bands = u_k.shape[2]
    width = bands * bands
    lanes = coarse.shape[3]
    mode_count = lanes // width
    modes = mode_count // lat_count
    cells = re_vectors.shape[0]
    rows = 2 * q_count * modes
    assert coarse.shape[1] == 1 and coarse.shape[2] == lat_count

    pr, pi = phases(q_points, rp_vectors, rp_weights)
    tail = jnp.concatenate(
        [jnp.concatenate([pr, pi], 1), jnp.concatenate([-pi, pr], 1)], 0
    )
    tail = jnp.pad(tail, ((0, 0), (0, 128 - 2 * q_count)))
    block = jnp.transpose(coarse[:, 0], (1, 0, 2))
    sent = jnp.concatenate([block, jnp.broadcast_to(tail[None], (lat_count, 2, 128))], 2)
    got = lax.all_to_all(sent, "lat", split_axis=0, concat_axis=0, tiled=True)
    got = got.reshape(2 * lat_count, lanes + 128)

    rr, ri = modes_rot[0], modes_rot[1]
    turn = jnp.stack([jnp.stack([rr, -ri]), jnp.stack([ri, rr])])
    turn = turn.reshape(2, 2, q_count, mode_count, lat_count, modes)
    same = jnp.eye(q_count, dtype=bf16)
    turn = turn[:, :, :, :, :, :, None] * same[None, None, :, None, None, None, :]
    turn = jnp.transpose(turn, (4, 6, 0, 5, 1, 2, 3)).reshape(
        lat_count * rows, 2 * q_count * mode_count
    )
    branch = pl.pallas_call(
        functools.partial(rotate_kernel, lanes, width),
        out_shape=jax.ShapeDtypeStruct((lat_count * rows, width), bf16),
        scratch_shapes=[pltpu.VMEM((2 * q_count * mode_count, width), f32)],
    )(got, turn)
    branch = branch.reshape(lat_count, rows, width)
    shared = lax.all_to_all(branch, "lat", split_axis=0, concat_axis=0, tiled=True)
    portion = lax.all_gather(shared, "kpt", axis=0, tiled=True).reshape(cells * rows, width)

    kr, ki = phases(k_points, re_vectors, re_weights)
    ph = jnp.concatenate(
        [jnp.concatenate([kr, ki], 1), jnp.concatenate([-ki, kr], 1)], 0
    )
    uk = jnp.transpose(u_k.astype(f32) * mask_k.astype(f32)[None, :, None, :], (0, 2, 3, 1))
    uk = uk.reshape(2, width, k_count)
    u1 = jnp.concatenate([uk[0], uk[0]], 1).astype(bf16)
    u2 = jnp.concatenate([-uk[1], uk[1]], 1).astype(bf16)
    ukq = jnp.transpose(u_kq.astype(f32) * mask_kq.astype(f32)[None, :, :, None, :], (0, 1, 3, 4, 2))
    ukq = ukq.reshape(2, q_count, width, k_count)
    v1 = jnp.concatenate([ukq[0], ukq[0]], 2)
    v2 = jnp.concatenate([ukq[1], -ukq[1]], 2)

    wide_lanes = 2 * k_count
    whole = lambda q, m: (0, 0)
    result = pl.pallas_call(
        functools.partial(couple_kernel, cells, modes, rows, bands),
        grid=(q_count, modes),
        in_specs=[
            pl.BlockSpec((cells * rows, width), whole),
            pl.BlockSpec((2 * cells, wide_lanes), whole),
            pl.BlockSpec((width, wide_lanes), whole),
            pl.BlockSpec((width, wide_lanes), whole),
            pl.BlockSpec((1, width, wide_lanes), lambda q, m: (q, 0, 0)),
            pl.BlockSpec((1, width, wide_lanes), lambda q, m: (q, 0, 0)),
        ],
        out_specs=pl.BlockSpec((1, wide_lanes, width), lambda q, m: (q, 0, m)),
        out_shape=jax.ShapeDtypeStruct((q_count, wide_lanes, modes * width), bf16),
        scratch_shapes=[pltpu.VMEM((width // 128, cells * rows, 128), f32)]
        + [pltpu.VMEM((width, wide_lanes), f32)] * 2
        + [pltpu.VMEM((width, wide_lanes), bf16)] * 2
        + [pltpu.VMEM((width, wide_lanes), f32)]
        + [pltpu.VMEM((width * bands, wide_lanes), bf16)] * 2,
    )(portion, ph, u1, u2, v1, v2)
    result = result.reshape(q_count, 2, k_count, modes * width)
    return jnp.transpose(result, (1, 2, 0, 3))


def solution(mesh):
    placed = (
        P(None, "lat", "kpt", None),
        P("lat", None),
        P("lat"),
        P(),
        P(),
        P(),
        P("kpt", None),
        P(),
        P(None, "kpt", None, None),
        P(None, None, "kpt", None, None),
        P("kpt", None),
        P(None, "kpt", None),
    )
    return jax.shard_map(
        functools.partial(per_device, mesh.shape["lat"], mesh.shape["kpt"]),
        mesh=mesh,
        in_specs=placed,
        out_specs=P(None, "kpt", None, "lat"),
        check_vma=False,
    )
```

```python
import functools

import jax
import jax.numpy as jnp
from jax import lax
from jax.experimental import pallas as pl
from jax.experimental.pallas import tpu as pltpu
from jax.sharding import PartitionSpec as P

two_pi = 6.283185307179586
f32 = jnp.float32
bf16 = jnp.bfloat16
MESH = pl.DeviceIdType.MESH


def phases(points, vectors, weights):
    cells = vectors.astype(f32)
    argument = two_pi * (
        points[None, :, 0] * cells[:, 0:1]
        + points[None, :, 1] * cells[:, 1:2]
        + points[None, :, 2] * cells[:, 2:3]
    )
    inverse = (1.0 / weights.astype(f32))[:, None]
    return (
        (jnp.cos(argument) * inverse).astype(bf16),
        (jnp.sin(argument) * inverse).astype(bf16),
    )


def rotate_kernel(lanes, width, lat_count, kpt_count, x_ref, rot_ref, out_ref, rows_ref, branch, own_sem, lat_send, lat_recv, chip_send, chip_recv, pair_send, pair_recv):
    lat = lax.axis_index("lat")
    kpt = lax.axis_index("kpt")
    chips = kpt_count // 2
    chip = kpt // 2
    core = kpt - 2 * chip
    pair = 2 * chip + 1 - core

    def lat_peer(step):
        return lax.rem(lat + step, lat_count)

    def chip_peer(step):
        return lax.rem(chip + step, chips)

    barrier = pltpu.get_barrier_semaphore()
    for step in range(1, lat_count):
        pl.semaphore_signal(barrier, inc=1, device_id=(lat_peer(step), kpt), device_id_type=MESH)
    for step in range(1, chips):
        pl.semaphore_signal(barrier, inc=1, device_id=(lat, 2 * chip_peer(step) + core), device_id_type=MESH)
    pl.semaphore_signal(barrier, inc=1, device_id=(lat, pair), device_id_type=MESH)

    count = lanes // width
    out_rows = rows_ref.shape[0] // count
    tail = x_ref[:, lanes:].astype(f32).T[: max(8, out_rows)].astype(bf16)
    total = jnp.dot(tail, x_ref[:, :lanes], preferred_element_type=f32)
    for row in range(out_rows):
        for m in range(count):
            rows_ref[pl.ds(row * count + m, 1), :] = total[row : row + 1, m * width : (m + 1) * width]
    turned = jnp.dot(
        rot_ref[...], rows_ref[...].astype(bf16), preferred_element_type=f32
    ).astype(bf16)
    rows = branch.shape[1]
    for d in range(lat_count):
        branch[d] = turned[d * rows : (d + 1) * rows]

    pl.semaphore_wait(barrier, lat_count + chips - 1)

    def chunk(owner):
        return out_ref.at[pl.ds(owner * lat_count, lat_count)]

    first = []
    for step in range(1, lat_count):
        copy = pltpu.make_async_remote_copy(
            src_ref=branch.at[lat_peer(step)],
            dst_ref=out_ref.at[kpt * lat_count + lat],
            send_sem=lat_send.at[step],
            recv_sem=lat_recv.at[step],
            device_id=(lat_peer(step), kpt),
            device_id_type=MESH,
        )
        copy.start()
        first.append(copy)
    own = pltpu.make_async_copy(branch.at[lat], out_ref.at[kpt * lat_count + lat], own_sem)
    own.start()
    own.wait()
    for copy in first:
        copy.wait_recv()

    second = []
    for step in range(1, chips):
        copy = pltpu.make_async_remote_copy(
            src_ref=chunk(kpt),
            dst_ref=chunk(kpt),
            send_sem=chip_send.at[step],
            recv_sem=chip_recv.at[step],
            device_id=(lat, 2 * chip_peer(step) + core),
            device_id_type=MESH,
        )
        copy.start()
        second.append(copy)

    third = []
    for step in range(chips):
        source = 2 * lax.rem(chip + chips - step, chips) + core
        if step > 0:
            second[step - 1].wait_recv()
        copy = pltpu.make_async_remote_copy(
            src_ref=chunk(source),
            dst_ref=chunk(source),
            send_sem=pair_send.at[step],
            recv_sem=pair_recv.at[step],
            device_id=(lat, pair),
            device_id_type=MESH,
        )
        copy.start()
        third.append(copy)
    for copy in third:
        copy.wait_recv()
    for copy in first + second + third:
        copy.wait_send()


def couple_kernel(cells, modes, rows, bands, p_ref, ph_ref, u1_ref, u2_ref, v1_ref, v2_ref, out_ref, wide, b1, b2, h1, h2, res):
    q = pl.program_id(0)
    m = pl.program_id(1)
    half_lanes = b1.shape[1] // 2

    @pl.when((q == 0) & (m == 0))
    def _():
        for t in range(wide.shape[0]):
            wide[t] = p_ref[:, :, t * 128 : (t + 1) * 128].astype(f32).reshape(wide.shape[1:])

    start = q * (2 * modes) + m
    parts = [
        jnp.concatenate(
            [
                wide.at[t][pl.ds(start + c * modes, cells, stride=rows), :]
                for t in range(wide.shape[0])
            ],
            axis=1,
        )
        for c in range(2)
    ]
    pair = jnp.concatenate(parts, axis=0).astype(bf16)
    field = lax.dot_general(pair, ph_ref[...], (((0,), (0,)), ((), ())), preferred_element_type=f32)
    b1[...] = field
    b2[...] = pltpu.roll(field, half_lanes, 1)
    lanes = b1.shape[1]
    group = 4

    def step_half(g, carry):
        base = g * (group * bands)
        acc = [jnp.zeros((bands, lanes), f32) for _ in range(group)]
        for b in range(bands):
            w1 = u1_ref[b * bands : (b + 1) * bands, :]
            w2 = u2_ref[b * bands : (b + 1) * bands, :]
            for j in range(group):
                r1 = b1[pl.ds(base + j * bands + b, 1), :]
                r2 = b2[pl.ds(base + j * bands + b, 1), :]
                acc[j] = acc[j] + (w1 * r1 + w2 * r2)
        for j in range(group):
            rows_at = pl.ds(pl.multiple_of(base + j * bands, bands), bands)
            h1[rows_at, :] = acc[j]
            h2[rows_at, :] = pltpu.roll(acc[j], half_lanes, 1)
        return carry

    lax.fori_loop(0, bands // group, step_half, 0)

    def step_out(g, carry):
        base = g * group
        acc = [jnp.zeros((bands, lanes), f32) for _ in range(group)]
        for a in range(bands):
            w1 = h1[a * bands : (a + 1) * bands, :]
            w2 = h2[a * bands : (a + 1) * bands, :]
            for j in range(group):
                r1 = v1_ref[0, pl.ds(a * bands + base + j, 1), :]
                r2 = v2_ref[0, pl.ds(a * bands + base + j, 1), :]
                acc[j] = acc[j] + (w1 * r1 + w2 * r2)
        for j in range(group):
            res[pl.ds(pl.multiple_of((base + j) * bands, bands), bands), :] = acc[j]
        return carry

    lax.fori_loop(0, bands // group, step_out, 0)
    out_ref[0] = res[...].T.astype(bf16)


def per_device(
    lat_count,
    kpt_count,
    coarse,
    rp_vectors,
    rp_weights,
    re_vectors,
    re_weights,
    q_points,
    k_points,
    modes_rot,
    u_k,
    u_kq,
    mask_k,
    mask_kq,
):
    q_count = q_points.shape[0]
    k_count = k_points.shape[0]
    bands = u_k.shape[2]
    width = bands * bands
    lanes = coarse.shape[3]
    mode_count = lanes // width
    modes = mode_count // lat_count
    cells = re_vectors.shape[0]
    rows = 2 * q_count * modes
    assert coarse.shape[1] == 1 and coarse.shape[2] == lat_count

    pr, pi = phases(q_points, rp_vectors, rp_weights)
    tail = jnp.concatenate(
        [jnp.concatenate([pr, pi], 1), jnp.concatenate([-pi, pr], 1)], 0
    )
    tail = jnp.pad(tail, ((0, 0), (0, 128 - 2 * q_count)))
    block = jnp.transpose(coarse[:, 0], (1, 0, 2))
    sent = jnp.concatenate([block, jnp.broadcast_to(tail[None], (lat_count, 2, 128))], 2)
    got = lax.all_to_all(sent, "lat", split_axis=0, concat_axis=0, tiled=True)
    got = got.reshape(2 * lat_count, lanes + 128)

    rr, ri = modes_rot[0], modes_rot[1]
    turn = jnp.stack([jnp.stack([rr, -ri]), jnp.stack([ri, rr])])
    turn = turn.reshape(2, 2, q_count, mode_count, lat_count, modes)
    same = jnp.eye(q_count, dtype=bf16)
    turn = turn[:, :, :, :, :, :, None] * same[None, None, :, None, None, None, :]
    turn = jnp.transpose(turn, (4, 6, 0, 5, 1, 2, 3)).reshape(
        lat_count, rows, 2 * q_count * mode_count
    )
    padded = -(-rows // 16) * 16
    turn = jnp.pad(turn, ((0, 0), (0, padded - rows), (0, 0)))
    turn = turn.reshape(lat_count * padded, 2 * q_count * mode_count)
    chips = kpt_count // 2
    dma = pltpu.SemaphoreType.DMA
    portion = pl.pallas_call(
        functools.partial(rotate_kernel, lanes, width, lat_count, kpt_count),
        in_specs=[pl.BlockSpec(memory_space=pltpu.VMEM)] * 2,
        out_specs=pl.BlockSpec(memory_space=pl.ANY),
        out_shape=jax.ShapeDtypeStruct((cells, padded, width), bf16),
        scratch_shapes=[
            pltpu.VMEM((2 * q_count * mode_count, width), f32),
            pltpu.VMEM((lat_count, padded, width), bf16),
            dma,
            dma((lat_count,)),
            dma((lat_count,)),
            dma((chips,)),
            dma((chips,)),
            dma((chips,)),
            dma((chips,)),
        ],
        compiler_params=pltpu.CompilerParams(collective_id=0, has_side_effects=True),
    )(got, turn)

    kr, ki = phases(k_points, re_vectors, re_weights)
    ph = jnp.concatenate(
        [jnp.concatenate([kr, ki], 1), jnp.concatenate([-ki, kr], 1)], 0
    )
    uk = jnp.transpose(u_k.astype(f32) * mask_k.astype(f32)[None, :, None, :], (0, 2, 3, 1))
    uk = uk.reshape(2, width, k_count)
    u1 = jnp.concatenate([uk[0], uk[0]], 1)
    u2 = jnp.concatenate([-uk[1], uk[1]], 1)
    ukq = jnp.transpose(u_kq.astype(f32) * mask_kq.astype(f32)[None, :, :, None, :], (0, 1, 3, 4, 2))
    ukq = ukq.reshape(2, q_count, width, k_count)
    v1 = jnp.concatenate([ukq[0], ukq[0]], 2)
    v2 = jnp.concatenate([ukq[1], -ukq[1]], 2)

    wide_lanes = 2 * k_count
    whole = lambda q, m: (0, 0)
    result = pl.pallas_call(
        functools.partial(couple_kernel, cells, modes, padded, bands),
        grid=(q_count, modes),
        in_specs=[
            pl.BlockSpec((cells, padded, width), lambda q, m: (0, 0, 0)),
            pl.BlockSpec((2 * cells, wide_lanes), whole),
            pl.BlockSpec((width, wide_lanes), whole),
            pl.BlockSpec((width, wide_lanes), whole),
            pl.BlockSpec((1, width, wide_lanes), lambda q, m: (q, 0, 0)),
            pl.BlockSpec((1, width, wide_lanes), lambda q, m: (q, 0, 0)),
        ],
        out_specs=pl.BlockSpec((1, wide_lanes, width), lambda q, m: (q, 0, m)),
        out_shape=jax.ShapeDtypeStruct((q_count, wide_lanes, modes * width), bf16),
        scratch_shapes=[pltpu.VMEM((width // 128, cells * padded, 128), f32)]
        + [pltpu.VMEM((width, wide_lanes), f32)] * 5,
    )(portion, ph, u1, u2, v1, v2)
    result = result.reshape(q_count, 2, k_count, modes * width)
    return jnp.transpose(result, (1, 2, 0, 3))


def solution(mesh):
    placed = (
        P(None, "lat", "kpt", None),
        P("lat", None),
        P("lat"),
        P(),
        P(),
        P(),
        P("kpt", None),
        P(),
        P(None, "kpt", None, None),
        P(None, None, "kpt", None, None),
        P("kpt", None),
        P(None, "kpt", None),
    )
    return jax.shard_map(
        functools.partial(per_device, mesh.shape["lat"], mesh.shape["kpt"]),
        mesh=mesh,
        in_specs=placed,
        out_specs=P(None, "kpt", None, "lat"),
        check_vma=False,
    )
```

```python
import functools

import jax
import jax.numpy as jnp
from jax import lax
from jax.experimental import pallas as pl
from jax.experimental.pallas import tpu as pltpu
from jax.sharding import PartitionSpec as P

two_pi = 6.283185307179586
f32 = jnp.float32
bf16 = jnp.bfloat16
MESH = pl.DeviceIdType.MESH


def phases(points, vectors, weights):
    cells = vectors.astype(f32)
    argument = two_pi * (
        points[None, :, 0] * cells[:, 0:1]
        + points[None, :, 1] * cells[:, 1:2]
        + points[None, :, 2] * cells[:, 2:3]
    )
    inverse = (1.0 / weights.astype(f32))[:, None]
    return (
        (jnp.cos(argument) * inverse).astype(bf16),
        (jnp.sin(argument) * inverse).astype(bf16),
    )


def rotate_kernel(lanes, width, lat_count, kpt_count, x_ref, rot_ref, out_ref, rows_ref, branch, own_sem, lat_send, lat_recv, chip_send, chip_recv, pair_send, pair_recv):
    lat = lax.axis_index("lat")
    kpt = lax.axis_index("kpt")
    chips = kpt_count // 2
    chip = kpt // 2
    core = kpt - 2 * chip
    pair = 2 * chip + 1 - core

    def lat_peer(step):
        return lax.rem(lat + step, lat_count)

    def chip_peer(step):
        return lax.rem(chip + step, chips)

    barrier = pltpu.get_barrier_semaphore()
    for step in range(1, lat_count):
        pl.semaphore_signal(barrier, inc=1, device_id=(lat_peer(step), kpt), device_id_type=MESH)
    for step in range(1, chips):
        pl.semaphore_signal(barrier, inc=1, device_id=(lat, 2 * chip_peer(step) + core), device_id_type=MESH)
    pl.semaphore_signal(barrier, inc=1, device_id=(lat, pair), device_id_type=MESH)

    count = lanes // width
    out_rows = rows_ref.shape[0] // count
    tail = x_ref[:, lanes:].astype(f32).T[: max(8, out_rows)].astype(bf16)
    total = jnp.dot(tail, x_ref[:, :lanes], preferred_element_type=f32)
    for row in range(out_rows):
        for m in range(count):
            rows_ref[pl.ds(row * count + m, 1), :] = total[row : row + 1, m * width : (m + 1) * width]
    turned = jnp.dot(
        rot_ref[...], rows_ref[...].astype(bf16), preferred_element_type=f32
    ).astype(bf16)
    rows = branch.shape[1]
    for d in range(lat_count):
        branch[d] = turned[d * rows : (d + 1) * rows]

    pl.semaphore_wait(barrier, lat_count + chips - 1)

    def chunk(owner):
        return out_ref.at[pl.ds(owner * lat_count, lat_count)]

    first = []
    for step in range(1, lat_count):
        copy = pltpu.make_async_remote_copy(
            src_ref=branch.at[lat_peer(step)],
            dst_ref=out_ref.at[kpt * lat_count + lat],
            send_sem=lat_send.at[step],
            recv_sem=lat_recv.at[step],
            device_id=(lat_peer(step), kpt),
            device_id_type=MESH,
        )
        copy.start()
        first.append(copy)
    own = pltpu.make_async_copy(branch.at[lat], out_ref.at[kpt * lat_count + lat], own_sem)
    own.start()
    own.wait()
    for copy in first:
        copy.wait_recv()

    second = []
    for step in range(1, chips):
        copy = pltpu.make_async_remote_copy(
            src_ref=chunk(kpt),
            dst_ref=chunk(kpt),
            send_sem=chip_send.at[step],
            recv_sem=chip_recv.at[step],
            device_id=(lat, 2 * chip_peer(step) + core),
            device_id_type=MESH,
        )
        copy.start()
        second.append(copy)

    third = []
    for step in range(chips):
        source = 2 * lax.rem(chip + chips - step, chips) + core
        if step > 0:
            second[step - 1].wait_recv()
        copy = pltpu.make_async_remote_copy(
            src_ref=chunk(source),
            dst_ref=chunk(source),
            send_sem=pair_send.at[step],
            recv_sem=pair_recv.at[step],
            device_id=(lat, pair),
            device_id_type=MESH,
        )
        copy.start()
        third.append(copy)
    for copy in third:
        copy.wait_recv()
    for copy in first + second + third:
        copy.wait_send()


def couple_kernel(cells, modes, rows, bands, p_ref, k_ref, u_ref, v_ref, out_ref, wide, ph, us, vs, bs, hs, res):
    m = pl.program_id(0)
    lanes = us.shape[2]
    q_count, k_count = v_ref.shape[1], v_ref.shape[3]

    def tile(index):
        return pl.ds(pl.multiple_of(index * bands, bands), bands)

    @pl.when(m == 0)
    def _():
        for t in range(wide.shape[0]):
            wide[t] = p_ref[:, :, t * 128 : (t + 1) * 128].astype(f32).reshape(wide.shape[1:])
        row = lax.broadcasted_iota(jnp.int32, (k_count, lanes), 0)
        col = lax.broadcasted_iota(jnp.int32, (k_count, lanes), 1)
        place = [(col == row * q_count + q).astype(f32).astype(bf16) for q in range(q_count)]

        def put(value, q):
            return jnp.dot(value, place[q], preferred_element_type=f32)

        for q in range(q_count):
            re, im = put(k_ref[0], q), put(k_ref[1], q)
            at = 2 * q * cells
            ph[at : at + cells, :lanes] = re.astype(bf16)
            ph[at : at + cells, lanes:] = im.astype(bf16)
            ph[at + cells : at + 2 * cells, :lanes] = (-im).astype(bf16)
            ph[at + cells : at + 2 * cells, lanes:] = re.astype(bf16)
        re = sum(put(u_ref[0], q) for q in range(q_count))
        im = sum(put(u_ref[1], q) for q in range(q_count))
        us[0], us[1], us[2] = re, im - re, re + im
        re = sum(put(v_ref[0, q], q) for q in range(q_count))
        im = -sum(put(v_ref[1, q], q) for q in range(q_count))
        vs[0], vs[1], vs[2] = re, im - re, re + im

    parts = [
        jnp.concatenate(
            [
                wide.at[t][pl.ds((2 * q + c) * modes + m, cells, stride=rows), :]
                for t in range(wide.shape[0])
            ],
            axis=1,
        )
        for q in range(q_count)
        for c in range(2)
    ]
    pair = jnp.concatenate(parts, axis=0).astype(bf16)
    field = lax.dot_general(pair, ph[...], (((0,), (0,)), ((), ())), preferred_element_type=f32)
    bs[1] = field[:, :lanes]
    bs[2] = field[:, lanes:]
    bs[0] = field[:, :lanes] + field[:, lanes:]
    group = 4

    def step_half(g, carry):
        base = g * (group * bands)
        acc = [[jnp.zeros((bands, lanes), f32)] * 3 for _ in range(group)]
        for b in range(bands):
            w = [us[t, b * bands : (b + 1) * bands, :] for t in range(3)]
            for j in range(group):
                r = base + j * bands + b
                acc[j] = [acc[j][t] + w[t] * bs[t, pl.ds(r, 1), :] for t in range(3)]
        for j in range(group):
            at = tile(g * group + j)
            re, im = acc[j][0] - acc[j][2], acc[j][0] + acc[j][1]
            hs[0, at, :], hs[1, at, :], hs[2, at, :] = re + im, re, im
        return carry

    lax.fori_loop(0, bands // group, step_half, 0)

    def step_out(g, carry):
        base = g * group
        acc = [[jnp.zeros((bands, lanes), f32)] * 3 for _ in range(group)]
        for a in range(bands):
            w = [hs[t, a * bands : (a + 1) * bands, :] for t in range(3)]
            for j in range(group):
                r = a * bands + base + j
                acc[j] = [acc[j][t] + w[t] * vs[t, pl.ds(r, 1), :] for t in range(3)]
        for j in range(group):
            at = tile(base + j)
            res[0, at, :], res[1, at, :] = acc[j][0] - acc[j][2], acc[j][0] + acc[j][1]
        return carry

    lax.fori_loop(0, bands // group, step_out, 0)
    for c in range(2):
        out_ref[c] = res[c].T.reshape(out_ref.shape[1:]).astype(bf16)


def per_device(
    lat_count,
    kpt_count,
    coarse,
    rp_vectors,
    rp_weights,
    re_vectors,
    re_weights,
    q_points,
    k_points,
    modes_rot,
    u_k,
    u_kq,
    mask_k,
    mask_kq,
):
    q_count = q_points.shape[0]
    k_count = k_points.shape[0]
    bands = u_k.shape[2]
    width = bands * bands
    lanes = coarse.shape[3]
    mode_count = lanes // width
    modes = mode_count // lat_count
    cells = re_vectors.shape[0]
    rows = 2 * q_count * modes
    assert coarse.shape[1] == 1 and coarse.shape[2] == lat_count

    pr, pi = phases(q_points, rp_vectors, rp_weights)
    tail = jnp.concatenate(
        [jnp.concatenate([pr, pi], 1), jnp.concatenate([-pi, pr], 1)], 0
    )
    tail = jnp.pad(tail, ((0, 0), (0, 128 - 2 * q_count)))
    block = jnp.transpose(coarse[:, 0], (1, 0, 2))
    sent = jnp.concatenate([block, jnp.broadcast_to(tail[None], (lat_count, 2, 128))], 2)
    got = lax.all_to_all(sent, "lat", split_axis=0, concat_axis=0, tiled=True)
    got = got.reshape(2 * lat_count, lanes + 128)

    rr, ri = modes_rot[0], modes_rot[1]
    turn = jnp.stack([jnp.stack([rr, -ri]), jnp.stack([ri, rr])])
    turn = turn.reshape(2, 2, q_count, mode_count, lat_count, modes)
    same = jnp.eye(q_count, dtype=bf16)
    turn = turn[:, :, :, :, :, :, None] * same[None, None, :, None, None, None, :]
    turn = jnp.transpose(turn, (4, 6, 0, 5, 1, 2, 3)).reshape(
        lat_count, rows, 2 * q_count * mode_count
    )
    padded = -(-rows // 16) * 16
    turn = jnp.pad(turn, ((0, 0), (0, padded - rows), (0, 0)))
    turn = turn.reshape(lat_count * padded, 2 * q_count * mode_count)
    chips = kpt_count // 2
    dma = pltpu.SemaphoreType.DMA
    portion = pl.pallas_call(
        functools.partial(rotate_kernel, lanes, width, lat_count, kpt_count),
        in_specs=[pl.BlockSpec(memory_space=pltpu.VMEM)] * 2,
        out_specs=pl.BlockSpec(memory_space=pl.ANY),
        out_shape=jax.ShapeDtypeStruct((cells, padded, width), bf16),
        scratch_shapes=[
            pltpu.VMEM((2 * q_count * mode_count, width), f32),
            pltpu.VMEM((lat_count, padded, width), bf16),
            dma,
            dma((lat_count,)),
            dma((lat_count,)),
            dma((chips,)),
            dma((chips,)),
            dma((chips,)),
            dma((chips,)),
        ],
        compiler_params=pltpu.CompilerParams(collective_id=0, has_side_effects=True),
    )(got, turn)

    kr, ki = phases(k_points, re_vectors, re_weights)
    waves = jnp.stack([kr, ki])
    uk = jnp.transpose(u_k * mask_k.astype(bf16)[None, :, None, :], (0, 2, 3, 1))
    uk = uk.reshape(2, width, k_count)
    ukq = jnp.transpose(u_kq * mask_kq.astype(bf16)[None, :, :, None, :], (0, 1, 3, 4, 2))
    ukq = ukq.reshape(2, q_count, width, k_count)

    wide_lanes = q_count * k_count
    fixed = lambda array: pl.BlockSpec(array.shape, lambda m: (0,) * array.ndim)
    return pl.pallas_call(
        functools.partial(couple_kernel, cells, modes, padded, bands),
        grid=(modes,),
        in_specs=[fixed(portion), fixed(waves), fixed(uk), fixed(ukq)],
        out_specs=pl.BlockSpec((2, k_count, q_count, width), lambda m: (0, 0, 0, m)),
        out_shape=jax.ShapeDtypeStruct((2, k_count, q_count, modes * width), bf16),
        scratch_shapes=[
            pltpu.VMEM((width // 128, cells * padded, 128), f32),
            pltpu.VMEM((2 * q_count * cells, 2 * wide_lanes), bf16),
            pltpu.VMEM((3, width, wide_lanes), f32),
            pltpu.VMEM((3, width, wide_lanes), f32),
            pltpu.VMEM((3, width, wide_lanes), f32),
            pltpu.VMEM((3, width, wide_lanes), f32),
            pltpu.VMEM((2, width, wide_lanes), f32),
        ],
    )(portion, waves, uk, ukq)


def solution(mesh):
    placed = (
        P(None, "lat", "kpt", None),
        P("lat", None),
        P("lat"),
        P(),
        P(),
        P(),
        P("kpt", None),
        P(),
        P(None, "kpt", None, None),
        P(None, None, "kpt", None, None),
        P("kpt", None),
        P(None, "kpt", None),
    )
    return jax.shard_map(
        functools.partial(per_device, mesh.shape["lat"], mesh.shape["kpt"]),
        mesh=mesh,
        in_specs=placed,
        out_specs=P(None, "kpt", None, "lat"),
        check_vma=False,
    )
```

```python
import functools

import jax
import jax.numpy as jnp
from jax import lax
from jax.experimental import pallas as pl
from jax.experimental.pallas import tpu as pltpu
from jax.sharding import PartitionSpec as P

two_pi = 6.283185307179586
f32 = jnp.float32
bf16 = jnp.bfloat16
MESH = pl.DeviceIdType.MESH


def phases(points, vectors, weights):
    cells = vectors.astype(f32)
    argument = two_pi * (
        points[None, :, 0] * cells[:, 0:1]
        + points[None, :, 1] * cells[:, 1:2]
        + points[None, :, 2] * cells[:, 2:3]
    )
    inverse = (1.0 / weights.astype(f32))[:, None]
    return (
        (jnp.cos(argument) * inverse).astype(bf16),
        (jnp.sin(argument) * inverse).astype(bf16),
    )


def rotate_kernel(lanes, width, lat_count, kpt_count, x_ref, rot_ref, out_ref, rows_ref, branch, own_sem, lat_send, lat_recv, chip_send, chip_recv, pair_send, pair_recv):
    lat = lax.axis_index("lat")
    kpt = lax.axis_index("kpt")
    chips = kpt_count // 2
    chip = kpt // 2
    core = kpt - 2 * chip
    pair = 2 * chip + 1 - core

    def lat_peer(step):
        return lax.rem(lat + step, lat_count)

    def chip_peer(step):
        return lax.rem(chip + step, chips)

    barrier = pltpu.get_barrier_semaphore()
    for step in range(1, lat_count):
        pl.semaphore_signal(barrier, inc=1, device_id=(lat_peer(step), kpt), device_id_type=MESH)
    for step in range(1, chips):
        pl.semaphore_signal(barrier, inc=1, device_id=(lat, 2 * chip_peer(step) + core), device_id_type=MESH)
    pl.semaphore_signal(barrier, inc=1, device_id=(lat, pair), device_id_type=MESH)

    count = lanes // width
    out_rows = rows_ref.shape[0] // count
    tail = x_ref[:, lanes:].astype(f32).T[: max(8, out_rows)].astype(bf16)
    total = jnp.dot(tail, x_ref[:, :lanes], preferred_element_type=f32)
    for row in range(out_rows):
        for m in range(count):
            rows_ref[pl.ds(row * count + m, 1), :] = total[row : row + 1, m * width : (m + 1) * width]
    turned = jnp.dot(
        rot_ref[...], rows_ref[...].astype(bf16), preferred_element_type=f32
    ).astype(bf16)
    rows = branch.shape[1]
    for d in range(lat_count):
        branch[d] = turned[d * rows : (d + 1) * rows]

    pl.semaphore_wait(barrier, lat_count + chips - 1)

    def chunk(owner):
        return out_ref.at[pl.ds(owner * lat_count, lat_count)]

    first = []
    for step in range(1, lat_count):
        copy = pltpu.make_async_remote_copy(
            src_ref=branch.at[lat_peer(step)],
            dst_ref=out_ref.at[kpt * lat_count + lat],
            send_sem=lat_send.at[step],
            recv_sem=lat_recv.at[step],
            device_id=(lat_peer(step), kpt),
            device_id_type=MESH,
        )
        copy.start()
        first.append(copy)
    own = pltpu.make_async_copy(branch.at[lat], out_ref.at[kpt * lat_count + lat], own_sem)
    own.start()
    own.wait()
    for copy in first:
        copy.wait_recv()

    second = []
    for step in range(1, chips):
        copy = pltpu.make_async_remote_copy(
            src_ref=chunk(kpt),
            dst_ref=chunk(kpt),
            send_sem=chip_send.at[step],
            recv_sem=chip_recv.at[step],
            device_id=(lat, 2 * chip_peer(step) + core),
            device_id_type=MESH,
        )
        copy.start()
        second.append(copy)

    third = []
    for step in range(chips):
        source = 2 * lax.rem(chip + chips - step, chips) + core
        if step > 0:
            second[step - 1].wait_recv()
        copy = pltpu.make_async_remote_copy(
            src_ref=chunk(source),
            dst_ref=chunk(source),
            send_sem=pair_send.at[step],
            recv_sem=pair_recv.at[step],
            device_id=(lat, pair),
            device_id_type=MESH,
        )
        copy.start()
        third.append(copy)
    for copy in third:
        copy.wait_recv()
    for copy in first + second + third:
        copy.wait_send()


def couple_kernel(cells, modes, rows, bands, p_ref, kr_ref, ki_ref, u_ref, v_ref, mk_ref, mkq_ref, out_ref, wide, ph, us, vs, bs, hs, res):
    m = pl.program_id(0)
    lanes = us.shape[2]
    q_count, k_count = v_ref.shape[1], v_ref.shape[3]

    def tile(index):
        return pl.ds(pl.multiple_of(index * bands, bands), bands)

    @pl.when(m == 0)
    def _():
        for t in range(wide.shape[0]):
            wide[t] = p_ref[:, :, t * 128 : (t + 1) * 128].astype(f32).reshape(wide.shape[1:])
        row = lax.broadcasted_iota(jnp.int32, (k_count, lanes), 0)
        col = lax.broadcasted_iota(jnp.int32, (k_count, lanes), 1)
        place = [(col == row * q_count + q).astype(f32).astype(bf16) for q in range(q_count)]

        def put(value, q):
            return jnp.dot(value, place[q], preferred_element_type=f32)

        for q in range(q_count):
            re, im = put(kr_ref[...], q), put(ki_ref[...], q)
            at = 2 * q * cells
            ph[at : at + cells, :lanes] = re.astype(bf16)
            ph[at : at + cells, lanes:] = im.astype(bf16)
            ph[at + cells : at + 2 * cells, :lanes] = (-im).astype(bf16)
            ph[at + cells : at + 2 * cells, lanes:] = re.astype(bf16)
        keep = sum(put(mk_ref[...].astype(f32).astype(bf16), q) for q in range(q_count))
        keep = jnp.concatenate([keep] * bands, axis=0)
        re = sum(put(u_ref[0], q) for q in range(q_count)) * keep
        im = sum(put(u_ref[1], q) for q in range(q_count)) * keep
        us[0], us[1], us[2] = re, im - re, re + im
        keep = sum(put(mkq_ref[q].astype(f32).astype(bf16), q) for q in range(q_count))
        keep = jnp.concatenate([keep] * bands, axis=0)
        re = sum(put(v_ref[0, q], q) for q in range(q_count)) * keep
        im = -sum(put(v_ref[1, q], q) for q in range(q_count)) * keep
        vs[0], vs[1], vs[2] = re, im - re, re + im

    parts = [
        jnp.concatenate(
            [
                wide.at[t][pl.ds((2 * q + c) * modes + m, cells, stride=rows), :]
                for t in range(wide.shape[0])
            ],
            axis=1,
        )
        for q in range(q_count)
        for c in range(2)
    ]
    pair = jnp.concatenate(parts, axis=0).astype(bf16)
    field = lax.dot_general(pair, ph[...], (((0,), (0,)), ((), ())), preferred_element_type=f32)
    bs[1] = field[:, :lanes]
    bs[2] = field[:, lanes:]
    bs[0] = field[:, :lanes] + field[:, lanes:]
    group = 4

    def step_half(g, carry):
        base = g * (group * bands)
        acc = [[jnp.zeros((bands, lanes), f32)] * 3 for _ in range(group)]
        for b in range(bands):
            w = [us[t, b * bands : (b + 1) * bands, :] for t in range(3)]
            for j in range(group):
                r = base + j * bands + b
                acc[j] = [acc[j][t] + w[t] * bs[t, pl.ds(r, 1), :] for t in range(3)]
        for j in range(group):
            at = tile(g * group + j)
            re, im = acc[j][0] - acc[j][2], acc[j][0] + acc[j][1]
            hs[0, at, :], hs[1, at, :], hs[2, at, :] = re + im, re, im
        return carry

    lax.fori_loop(0, bands // group, step_half, 0)

    def step_out(g, carry):
        base = g * group
        acc = [[jnp.zeros((bands, lanes), f32)] * 3 for _ in range(group)]
        for a in range(bands):
            w = [hs[t, a * bands : (a + 1) * bands, :] for t in range(3)]
            for j in range(group):
                r = a * bands + base + j
                acc[j] = [acc[j][t] + w[t] * vs[t, pl.ds(r, 1), :] for t in range(3)]
        for j in range(group):
            at = tile(base + j)
            res[0, at, :], res[1, at, :] = acc[j][0] - acc[j][2], acc[j][0] + acc[j][1]
        return carry

    lax.fori_loop(0, bands // group, step_out, 0)
    for c in range(2):
        out_ref[c] = res[c].T.reshape(out_ref.shape[1:]).astype(bf16)


def per_device(
    lat_count,
    kpt_count,
    coarse,
    rp_vectors,
    rp_weights,
    re_vectors,
    re_weights,
    q_points,
    k_points,
    modes_rot,
    u_k,
    u_kq,
    mask_k,
    mask_kq,
):
    q_count = q_points.shape[0]
    k_count = k_points.shape[0]
    bands = u_k.shape[2]
    width = bands * bands
    lanes = coarse.shape[3]
    mode_count = lanes // width
    modes = mode_count // lat_count
    cells = re_vectors.shape[0]
    rows = 2 * q_count * modes
    assert coarse.shape[1] == 1 and coarse.shape[2] == lat_count

    pr, pi = phases(q_points, rp_vectors, rp_weights)
    tail = jnp.concatenate(
        [jnp.concatenate([pr, pi], 1), jnp.concatenate([-pi, pr], 1)], 0
    )
    tail = jnp.pad(tail, ((0, 0), (0, 128 - 2 * q_count)))
    block = jnp.transpose(coarse[:, 0], (1, 0, 2))
    sent = jnp.concatenate([block, jnp.broadcast_to(tail[None], (lat_count, 2, 128))], 2)
    got = lax.all_to_all(sent, "lat", split_axis=0, concat_axis=0, tiled=True)
    got = got.reshape(2 * lat_count, lanes + 128)

    rr, ri = modes_rot[0], modes_rot[1]
    turn = jnp.stack([jnp.stack([rr, -ri]), jnp.stack([ri, rr])])
    turn = turn.reshape(2, 2, q_count, mode_count, lat_count, modes)
    same = jnp.eye(q_count, dtype=bf16)
    turn = turn[:, :, :, :, :, :, None] * same[None, None, :, None, None, None, :]
    turn = jnp.transpose(turn, (4, 6, 0, 5, 1, 2, 3)).reshape(
        lat_count, rows, 2 * q_count * mode_count
    )
    padded = -(-rows // 16) * 16
    turn = jnp.pad(turn, ((0, 0), (0, padded - rows), (0, 0)))
    turn = turn.reshape(lat_count * padded, 2 * q_count * mode_count)
    chips = kpt_count // 2
    dma = pltpu.SemaphoreType.DMA
    portion = pl.pallas_call(
        functools.partial(rotate_kernel, lanes, width, lat_count, kpt_count),
        in_specs=[pl.BlockSpec(memory_space=pltpu.VMEM)] * 2,
        out_specs=pl.BlockSpec(memory_space=pl.ANY),
        out_shape=jax.ShapeDtypeStruct((cells, padded, width), bf16),
        scratch_shapes=[
            pltpu.VMEM((2 * q_count * mode_count, width), f32),
            pltpu.VMEM((lat_count, padded, width), bf16),
            dma,
            dma((lat_count,)),
            dma((lat_count,)),
            dma((chips,)),
            dma((chips,)),
            dma((chips,)),
            dma((chips,)),
        ],
        compiler_params=pltpu.CompilerParams(collective_id=0, has_side_effects=True),
    )(got, turn)

    kr, ki = phases(k_points, re_vectors, re_weights)
    uk = jnp.transpose(u_k, (0, 2, 3, 1)).reshape(2, width, k_count)
    ukq = jnp.transpose(u_kq, (0, 1, 3, 4, 2)).reshape(2, q_count, width, k_count)
    keep_k = jnp.transpose(mask_k)
    keep_kq = jnp.transpose(mask_kq, (0, 2, 1))

    wide_lanes = q_count * k_count
    fixed = lambda array: pl.BlockSpec(array.shape, lambda m: (0,) * array.ndim)
    return pl.pallas_call(
        functools.partial(couple_kernel, cells, modes, padded, bands),
        grid=(modes,),
        in_specs=[fixed(x) for x in (portion, kr, ki, uk, ukq, keep_k, keep_kq)],
        out_specs=pl.BlockSpec((2, k_count, q_count, width), lambda m: (0, 0, 0, m)),
        out_shape=jax.ShapeDtypeStruct((2, k_count, q_count, modes * width), bf16),
        scratch_shapes=[
            pltpu.VMEM((width // 128, cells * padded, 128), f32),
            pltpu.VMEM((2 * q_count * cells, 2 * wide_lanes), bf16),
            pltpu.VMEM((3, width, wide_lanes), f32),
            pltpu.VMEM((3, width, wide_lanes), f32),
            pltpu.VMEM((3, width, wide_lanes), f32),
            pltpu.VMEM((3, width, wide_lanes), f32),
            pltpu.VMEM((2, width, wide_lanes), f32),
        ],
    )(portion, kr, ki, uk, ukq, keep_k, keep_kq)


def solution(mesh):
    placed = (
        P(None, "lat", "kpt", None),
        P("lat", None),
        P("lat"),
        P(),
        P(),
        P(),
        P("kpt", None),
        P(),
        P(None, "kpt", None, None),
        P(None, None, "kpt", None, None),
        P("kpt", None),
        P(None, "kpt", None),
    )
    return jax.shard_map(
        functools.partial(per_device, mesh.shape["lat"], mesh.shape["kpt"]),
        mesh=mesh,
        in_specs=placed,
        out_specs=P(None, "kpt", None, "lat"),
        check_vma=False,
    )
```
